256 devices in a mesh: ctx: 32 (over y_lo, z, core), tp: 8 (over y_hi, x).
Axes of the slice: x: 4, y: 4 (y_hi: 2, y_lo: 2; y = y_hi * 2 + y_lo), z: 8, core: 2. Of those that a mesh axis runs over, the one named last changes fastest.
Arguments:
- tokens_clean: bfloat16 [4096, 4096], P(('ctx', 'tp')), may hold values from -6 to 6
- noise_mask: int32 [4096], P(('ctx', 'tp')), may hold values 0 or 1
- mask_embed: bfloat16 [4096], replicated, may hold values from -6 to 6
- norm_gain: bfloat16 [4096], replicated, may hold values from 0.099609375 to 1.8984375
- w_query: bfloat16 [4096, 2048], P(None, 'tp'), may hold values from -0.375 to 0.375
- w_key: bfloat16 [4096, 2048], P(None, 'tp'), may hold values from -0.375 to 0.375
- w_value: bfloat16 [4096, 2048], P(None, 'tp'), may hold values from -0.09375 to 0.09375
- w_out: bfloat16 [2048, 4096], P('tp'), may hold values from -0.5 to 0.5
- block_mask: int32 [128, 128], replicated, may hold values from 0 to 3, as said below
Outputs:
- clean_out: bfloat16 [4096, 4096], P(('ctx', 'tp'))
- noisy_out: bfloat16 [4096, 4096], P(('ctx', 'tp'))
The draws below stay inside these ranges and needn't reach their ends.
Inputs may be any that keep to these rules, and one draw needn't show every extreme that they name: `block_mask`: entry (i, j) is a + 2 b: a = 1 where clean block i sees clean block j, b = 1 where noisy block i sees clean block j. For each i the j with a = 1 form one run ending at j = i, and those with b = 1 one run ending at j = i - 1, or none; entries with j > i are 0.
All inputs are finite; a program needn't handle non-finite values. No bound on the sum of `noise_mask` on one device may be relied on, other than what follows from the above.
Results may differ from the reference program's by a relative error of at most 0.014.
Values may be sent and summed in bfloat16 or wider, within the bound.
No kernel may reach another device: no remote copies, remote signals or barrier semaphores. Data moves between devices by JAX's collectives and lax.ppermute only.
A program may use at most 128 MiB of HBM per device.

```python
import jax
import jax.numpy as jnp
from jax import lax

D = 4096
HEADS = 16
HEAD_DIM = 128
BLOCK = 32
TOK_DEV = 128
SEQ = 4096
NBLK = 128
N_TP = 8


def pair_weights(key):
    base = jax.random.normal(jax.random.fold_in(key, 11), (D, HEADS * HEAD_DIM), jnp.float32)
    other = jax.random.normal(jax.random.fold_in(key, 12), (D, HEADS * HEAD_DIM), jnp.float32)
    return (base, other)


def draw_w_query(key, part):
    base, other = pair_weights(key)
    weight = base * D ** (-0.5)
    return jnp.clip(weight, -0.375, 0.375).astype(jnp.bfloat16)


def draw_w_key(key, part):
    base, other = pair_weights(key)
    weight = other * D ** (-0.5)
    return jnp.clip(weight, -0.375, 0.375).astype(jnp.bfloat16)


def draw_block_mask(key, part):
    blocks = jnp.arange(NBLK, dtype=jnp.int32)
    clean_start = jax.random.randint(jax.random.fold_in(key, 21), (NBLK,), 0, blocks + 1)
    noisy_start = jax.random.randint(jax.random.fold_in(key, 22), (NBLK,), 0, blocks + 1)
    columns = blocks[None, :]
    clean = (columns >= clean_start[:, None]) & (columns <= blocks[:, None])
    noisy = (columns >= noisy_start[:, None]) & (columns < blocks[:, None])
    return clean.astype(jnp.int32) + 2 * noisy.astype(jnp.int32)


def place_ends(result, key, smallest, largest):
    longest = result.shape.index(max(result.shape))
    spots = []
    for shift in (0, 1):
        where = [jax.random.randint(jax.random.fold_in(key, axis), (), 0, length) for axis, length in enumerate(result.shape)]
        where[longest] = (where[longest] + shift) % result.shape[longest]
        spots.append(tuple(where))
    return result.at[spots[0]].set(smallest).at[spots[1]].set(largest)


def levels(stream_key, dims, cuts, low, high):
    def one(axis_at, blocks):
        draws = jax.random.uniform(jax.random.fold_in(jax.random.fold_in(stream_key, 6), axis_at), (blocks,), jnp.float32, low / len(cuts), high / len(cuts))
        return jnp.repeat(jnp.exp(draws), dims[axis_at] // blocks).reshape((-1,) + (1,) * (len(dims) - axis_at - 1))

    factor_of = one(*cuts[0])
    for cut in cuts[1:]:
        factor_of = factor_of * one(*cut)
    return factor_of


def scatter_about(rng, shape, deviation, reach, shards=(), kind=jnp.bfloat16):
    entries = jax.random.normal(rng, shape, jnp.float32) * deviation
    if len(shards) > 0:
        entries = levels(rng, shape, shards, -0.22, 0.18) * entries
    return jnp.clip(entries, min=-reach, max=reach).astype(kind)


def setup_inputs(seed: int = 0) -> dict:
    seeds = jax.random.split(jax.random.key(seed), 10)
    return {
        "tokens_clean": scatter_about(seeds[0], (SEQ, D), 1.0, 6.0, ((0, 256),)),
        "noise_mask": place_ends((jax.random.randint(seeds[1], (SEQ,), 0, 2) < 1).astype(jnp.int32), jax.random.fold_in(seeds[1], 1), 0, 1),
        "mask_embed": scatter_about(seeds[2], (D,), 1.0, 6.0),
        "norm_gain": jnp.clip(1.0 + 0.18 * jax.random.normal(seeds[3], (D,), jnp.float32), 0.099609375, 1.8984375).astype(jnp.bfloat16),
        "w_query": draw_w_query(jax.random.fold_in(seeds[9], 71), 0),
        "w_key": draw_w_key(jax.random.fold_in(seeds[9], 71), 0),
        "w_value": scatter_about(seeds[6], (D, HEADS * HEAD_DIM), D ** -0.5, 0.09375, ((1, 8),)),
        "w_out": scatter_about(seeds[7], (HEADS * HEAD_DIM, D), HEAD_DIM ** -0.5, 0.5, ((0, 8),)),
        "block_mask": draw_block_mask(jax.random.fold_in(seeds[9], 71), 0),
    }


ROPE_BASE = 500000.0
EPSILON = 1e-05

def rms_rows(values, gain):
    wide = values.astype(jnp.float32)
    factor = lax.rsqrt(lax.optimization_barrier(jnp.mean(wide * wide, axis=-1, keepdims=True)) + EPSILON)
    return (wide * factor * gain.astype(jnp.float32)).astype(jnp.bfloat16)

def rotate(values, positions):
    half_dim = values.shape[-1] // 2
    indices = jnp.arange(half_dim).astype(jnp.float32)
    freqs = ROPE_BASE ** (-2.0 * indices / values.shape[-1])
    angles = positions.astype(jnp.float32)[:, None] * freqs[None, :]
    cosine = jnp.cos(angles)[:, None, :]
    sine = jnp.sin(angles)[:, None, :]
    lower = values[..., :half_dim]
    upper = values[..., half_dim:]
    return jnp.concatenate([lower * cosine - upper * sine, upper * cosine + lower * sine], axis=-1)

def widen(values):
    return lax.optimization_barrier(values).astype(jnp.float32)

def mixed_softmax(scores, visible, values):
    masked = jnp.where(visible, scores, -jnp.inf)
    peak = lax.optimization_barrier(jnp.max(masked, axis=-1, keepdims=True))
    weights = jnp.where(visible, jnp.exp(scores - peak), 0.0)
    total = lax.optimization_barrier(jnp.sum(weights, axis=-1))
    weighted = jnp.einsum('hqk,khd->hqd', widen(weights.astype(jnp.bfloat16)), values)
    return jnp.transpose(weighted / total[..., None], (1, 0, 2))

def reference(tokens_clean, noise_mask, mask_embed, norm_gain, w_query, w_key, w_value, w_out, block_mask):
    normed = rms_rows(tokens_clean, norm_gain)
    mask_row = rms_rows(mask_embed[None, :], norm_gain)
    noisy_rows = (noise_mask == 1)[:, None]
    positions = jnp.arange(SEQ, dtype=jnp.int32)

    def project(weight, rotary):
        clean = jnp.dot(normed, weight, preferred_element_type=jnp.float32)
        masked = jnp.dot(mask_row, weight, preferred_element_type=jnp.float32)
        noisy = jnp.where(noisy_rows, masked, clean)
        clean = clean.reshape(SEQ, HEADS, HEAD_DIM)
        noisy = noisy.reshape(SEQ, HEADS, HEAD_DIM)
        if rotary:
            clean = rotate(clean, positions)
            noisy = rotate(noisy, positions)
        return (widen(clean.astype(jnp.bfloat16)), widen(noisy.astype(jnp.bfloat16)))
    q_clean, q_noisy = project(w_query, True)
    k_clean, k_noisy = project(w_key, True)
    v_clean, v_noisy = project(w_value, False)
    score_scale = HEAD_DIM ** (-0.5)
    key_blocks = positions // BLOCK

    def one_block(index):
        begin = index * TOK_DEV
        query_blocks = (begin + jnp.arange(TOK_DEV, dtype=jnp.int32)) // BLOCK
        table = jnp.take(block_mask, query_blocks, axis=0)
        visible = jnp.take(table, key_blocks, axis=1)
        clean_seen = visible % 2 == 1
        noisy_seen = visible // 2 == 1
        own_block = query_blocks[:, None] == query_blocks[None, :]
        query_clean = lax.dynamic_slice_in_dim(q_clean, begin, TOK_DEV, 0)
        query_noisy = lax.dynamic_slice_in_dim(q_noisy, begin, TOK_DEV, 0)
        key_own = lax.dynamic_slice_in_dim(k_noisy, begin, TOK_DEV, 0)
        value_own = lax.dynamic_slice_in_dim(v_noisy, begin, TOK_DEV, 0)
        clean_scores = jnp.einsum('qhd,khd->hqk', query_clean, k_clean) * score_scale
        out_clean = mixed_softmax(clean_scores, clean_seen[None], v_clean)
        noisy_scores = jnp.concatenate([jnp.einsum('qhd,khd->hqk', query_noisy, k_clean), jnp.einsum('qhd,khd->hqk', query_noisy, key_own)], axis=-1) * score_scale
        noisy_visible = jnp.concatenate([noisy_seen, own_block], axis=-1)[None]
        noisy_values = jnp.concatenate([v_clean, value_own], axis=0)
        out_noisy = mixed_softmax(noisy_scores, noisy_visible, noisy_values)
        return (out_clean.reshape(TOK_DEV, HEADS * HEAD_DIM).astype(jnp.bfloat16), out_noisy.reshape(TOK_DEV, HEADS * HEAD_DIM).astype(jnp.bfloat16))
    outs_clean, outs_noisy = lax.map(one_block, jnp.arange(SEQ // TOK_DEV, dtype=jnp.int32))
    outs_clean = outs_clean.reshape(SEQ, HEADS * HEAD_DIM)
    outs_noisy = outs_noisy.reshape(SEQ, HEADS * HEAD_DIM)
    group_width = HEADS * HEAD_DIM // N_TP

    def project_out(attended):
        total = jnp.zeros((SEQ, D), jnp.float32)
        for group in range(N_TP):
            part = jnp.dot(attended[:, group * group_width:(group + 1) * group_width], w_out[group * group_width:(group + 1) * group_width, :], preferred_element_type=jnp.float32)
            total = total + widen(part.astype(jnp.bfloat16))
        return total.astype(jnp.bfloat16)
    return (project_out(outs_clean), project_out(outs_noisy))
```

```python
import jax
import jax.numpy as jnp
from jax import lax
from jax.experimental import pallas as pl
from jax.experimental.pallas import tpu as pltpu
from jax.sharding import PartitionSpec as P

HEAD_DIM = 128
BLOCK = 32
ROPE_BASE = 500000.0
EPSILON = 1e-05
TOK = 128
D = 4096
NZ = 8
LOG2E = 1.4426950408889634
SCALE2 = HEAD_DIM ** (-0.5) * LOG2E
HIDDEN = -1e30
FLOOR = -1e29


VMEM = pl.BlockSpec(memory_space=pltpu.VMEM)
SMEM = pl.BlockSpec(memory_space=pltpu.SMEM)


def params():
    return pltpu.CompilerParams(vmem_limit_bytes=32 << 20)


def rms(values, gain):
    wide = values.astype(jnp.float32)
    factor = lax.rsqrt(jnp.mean(wide * wide, axis=-1, keepdims=True) + EPSILON)
    return (wide * factor * gain.astype(jnp.float32)).astype(jnp.bfloat16)


def norm_kernel(tok_ref, flag_ref, mask_ref, gain_ref, out_ref, mask_out_ref):
    gain = gain_ref[...]
    rows = rms(tok_ref[...], gain)
    flags = jnp.broadcast_to(flag_ref[...], (16, 128)).astype(jnp.float32).astype(jnp.bfloat16)
    for t in range(8):
        out_ref[t, :, :D] = rows
        out_ref[t, :, D:] = flags
    mask_out_ref[...] = jnp.broadcast_to(rms(mask_ref[...], gain), (16, D))


def norm(tokens, flags, mask_embed, gain):
    return pl.pallas_call(
        norm_kernel,
        out_shape=(
            jax.ShapeDtypeStruct((8, 16, D + 128), jnp.bfloat16),
            jax.ShapeDtypeStruct((16, D), jnp.bfloat16),
        ),
        in_specs=[VMEM] * 4,
        out_specs=(VMEM, VMEM),
        compiler_params=params(),
        cost_estimate=pl.CostEstimate(flops=1 << 20, bytes_accessed=3 << 20, transcendentals=0),
    )(tokens, flags.reshape(16, 1), mask_embed.reshape(1, D), gain.reshape(1, D))


def project_kernel(g_ref, m_ref, wq_ref, wk_ref, wv_ref, cos_ref, sin_ref, q_ref, kv_ref, kvn_ref):
    rows = g_ref[...].reshape(TOK, D + 128)
    lhs = rows[:, :D]
    noisy = rows[:, D : D + 1].astype(jnp.float32) > 0.5
    cosine = cos_ref[...]
    sine = sin_ref[...]
    mask = m_ref[...]

    def one(w_ref, rotary):
        w = w_ref[...]
        clean = jnp.dot(lhs, w, preferred_element_type=jnp.float32)
        masked = jnp.dot(mask, w, preferred_element_type=jnp.float32)[:1]
        mixed = jnp.where(noisy, masked, clean)
        outs = []
        for part in (clean, mixed):
            for h in range(2):
                v = part[:, h * HEAD_DIM : (h + 1) * HEAD_DIM]
                if rotary:
                    v = v * cosine + pltpu.roll(v, HEAD_DIM // 2, 1) * sine
                outs.append(v.astype(jnp.bfloat16))
        return outs

    q = one(wq_ref, True)
    k = one(wk_ref, True)
    v = one(wv_ref, False)
    for h in range(2):
        lanes = slice(h * HEAD_DIM, (h + 1) * HEAD_DIM)
        upper = slice(256 + h * HEAD_DIM, 256 + (h + 1) * HEAD_DIM)
        q_ref[:TOK, lanes] = q[h]
        q_ref[TOK:, lanes] = q[2 + h]
        kv_ref[:, lanes] = k[h]
        kv_ref[:, upper] = v[h]
        kvn_ref[:, lanes] = k[2 + h]
        kvn_ref[:, upper] = v[2 + h]


def project(gathered, mask_row, wq, wk, wv, cosine, sine):
    return pl.pallas_call(
        project_kernel,
        out_shape=(
            jax.ShapeDtypeStruct((2 * TOK, 256), jnp.bfloat16),
            jax.ShapeDtypeStruct((TOK, 512), jnp.bfloat16),
            jax.ShapeDtypeStruct((TOK, 512), jnp.bfloat16),
        ),
        in_specs=[VMEM] * 7,
        out_specs=(VMEM, VMEM, VMEM),
        compiler_params=params(),
        cost_estimate=pl.CostEstimate(flops=2 << 30, bytes_accessed=8 << 20, transcendentals=0),
    )(gathered, mask_row, wq, wk, wv, cosine, sine)


def pack_stats(lses):
    rows = lses[0].shape[0]
    lane = lax.broadcasted_iota(jnp.int32, (rows, 128), 1)
    total = jnp.zeros((rows, 128), jnp.float32)
    for h, lse in enumerate(lses):
        rest = lse
        for part in range(3):
            piece = rest.astype(jnp.bfloat16).astype(jnp.float32)
            total = jnp.where(lane == h * 4 + part, piece, total)
            rest = rest - piece
    return total.astype(jnp.bfloat16)


def unpack_stats(block):
    wide = block.astype(jnp.float32)
    return [
        wide[:, h * 4 : h * 4 + 1] + wide[:, h * 4 + 1 : h * 4 + 2] + wide[:, h * 4 + 2 : h * 4 + 3]
        for h in range(2)
    ]


def attend_kernel(*refs):
    where_ref, table_ref = refs[:2]
    q_refs = refs[2:6]
    kv_refs = refs[6:14]
    kvn_ref = refs[14]
    out_ref = refs[15]
    keys = refs[16]
    y, z, c = where_ref[0], where_ref[1], where_ref[2]
    for s in range(NZ):
        keys[s * TOK : (s + 1) * TOK, :] = kv_refs[s][...]
    col = lax.broadcasted_iota(jnp.int32, (1, NZ * TOK), 1)
    source = (z - col // TOK) & (NZ - 1)
    key_block = (y * 16 + source * 2 + c) * 4 + (col % TOK) // BLOCK
    row = lax.broadcasted_iota(jnp.int32, (2 * TOK, 1), 0)
    part = row // BLOCK
    for g in range(4):
        yq = y if g < 2 else 1
        cq = c if g % 2 == 0 else 1 - c
        first = (yq * 16 + z * 2 + cq) * 4
        low = jnp.zeros((2 * TOK, 1), jnp.int32)
        high = jnp.zeros((2 * TOK, 1), jnp.int32)
        for p in range(8):
            copy, block = p // 4, first + p % 4
            start = table_ref[copy, block]
            if g >= 2:
                start = jnp.where(y == 0, start, 1 << 20)
            low = jnp.where(part == p, start, low)
            high = jnp.where(part == p, block - copy, high)
        visible = (key_block >= low) & (key_block <= high)
        lses = []
        for h in range(2):
            lanes = slice(h * HEAD_DIM, (h + 1) * HEAD_DIM)
            upper = slice(256 + h * HEAD_DIM, 256 + (h + 1) * HEAD_DIM)
            q = q_refs[g][:, lanes]
            scores = lax.dot_general(
                q, keys[:, lanes], (((1,), (1,)), ((), ())), preferred_element_type=jnp.float32
            ) * SCALE2
            scores = jnp.where(visible, scores, HIDDEN)
            peak = jnp.maximum(jnp.max(scores, axis=-1, keepdims=True), FLOOR)
            if g == 0:
                own = lax.dot_general(
                    q[TOK:], kvn_ref[:, lanes], (((1,), (1,)), ((), ())),
                    preferred_element_type=jnp.float32,
                ) * SCALE2
                near = (
                    lax.broadcasted_iota(jnp.int32, (TOK, TOK), 0) // BLOCK
                    == lax.broadcasted_iota(jnp.int32, (TOK, TOK), 1) // BLOCK
                )
                own = jnp.where(near, own, HIDDEN)
                peak_own = jnp.maximum(peak[TOK:], jnp.max(own, axis=-1, keepdims=True))
                peak = jnp.concatenate([peak[:TOK], peak_own], axis=0)
            weights = jnp.exp2(scores - peak)
            total = jnp.sum(weights, axis=-1, keepdims=True)
            weighted = jnp.dot(
                weights.astype(jnp.bfloat16), keys[:, upper], preferred_element_type=jnp.float32
            )
            if g == 0:
                wown = jnp.exp2(own - peak_own)
                total = total + jnp.concatenate(
                    [jnp.zeros((TOK, 1), jnp.float32), jnp.sum(wown, axis=-1, keepdims=True)], axis=0
                )
                extra = jnp.dot(
                    wown.astype(jnp.bfloat16), kvn_ref[:, upper], preferred_element_type=jnp.float32
                )
                weighted = weighted + jnp.concatenate(
                    [jnp.zeros((TOK, HEAD_DIM), jnp.float32), extra], axis=0
                )
            some = total > 0.0
            safe = jnp.where(some, total, 1.0)
            out_ref[g, :, lanes] = (weighted / safe).astype(jnp.bfloat16)
            lses.append(jnp.where(some, peak + jnp.log2(safe), FLOOR))
        out_ref[g, :, 256:] = pack_stats(lses)


def attend(where, table, queries, key_values, own):
    return pl.pallas_call(
        attend_kernel,
        out_shape=jax.ShapeDtypeStruct((4, 2 * TOK, 384), jnp.bfloat16),
        in_specs=[SMEM, SMEM] + [VMEM] * 13,
        out_specs=VMEM,
        scratch_shapes=[pltpu.VMEM((NZ * TOK, 512), jnp.bfloat16)],
        compiler_params=params(),
        cost_estimate=pl.CostEstimate(flops=1 << 30, bytes_accessed=4 << 20, transcendentals=1 << 21),
    )(where, table, *queries, *key_values, own)


def merge(a, b):
    outs, lses = [], []
    sa, sb = unpack_stats(a[:, 256:]), unpack_stats(b[:, 256:])
    for h in range(2):
        lanes = slice(h * HEAD_DIM, (h + 1) * HEAD_DIM)
        peak = jnp.maximum(sa[h], sb[h])
        wa, wb = jnp.exp2(sa[h] - peak), jnp.exp2(sb[h] - peak)
        total = wa + wb
        outs.append((a[:, lanes].astype(jnp.float32) * wa + b[:, lanes].astype(jnp.float32) * wb) / total)
        lses.append(peak + jnp.log2(total))
    return outs, lses


def merge_kernel(mine_ref, swap_ref, self_ref, far_ref):
    for g, out_ref in ((0, self_ref), (2, far_ref)):
        outs, lses = merge(mine_ref[g], swap_ref[g // 2])
        for h in range(2):
            out_ref[:, h * HEAD_DIM : (h + 1) * HEAD_DIM] = outs[h].astype(jnp.bfloat16)
        out_ref[:, 256:] = pack_stats(lses)


def merge_cores(mine, swapped):
    shape = jax.ShapeDtypeStruct((2 * TOK, 384), jnp.bfloat16)
    return pl.pallas_call(
        merge_kernel,
        out_shape=(shape, shape),
        in_specs=[VMEM, VMEM],
        out_specs=(VMEM, VMEM),
        compiler_params=params(),
        cost_estimate=pl.CostEstimate(flops=1 << 20, bytes_accessed=1 << 20, transcendentals=0),
    )(mine, swapped)


def output_kernel(where_ref, self_ref, far_ref, w_ref, out_ref):
    far = far_ref[...]
    outs, _ = merge(self_ref[...], far)
    upper_line = where_ref[0] == 1
    for h in range(2):
        alone = self_ref[:, h * HEAD_DIM : (h + 1) * HEAD_DIM].astype(jnp.float32)
        outs[h] = jnp.where(upper_line, outs[h], alone)
    attended = jnp.concatenate(outs, axis=1).astype(jnp.bfloat16)
    terms = jnp.dot(attended, w_ref[...], preferred_element_type=jnp.float32).astype(jnp.bfloat16)
    for t in range(8):
        for s in range(2):
            out_ref[t, s * 16 : (s + 1) * 16, :] = terms[s * TOK + t * 16 : s * TOK + (t + 1) * 16]


def output(where, mine, far, w_out):
    tile = 512
    return pl.pallas_call(
        output_kernel,
        grid=(D // tile,),
        out_shape=jax.ShapeDtypeStruct((8, 32, D), jnp.bfloat16),
        in_specs=[
            SMEM,
            pl.BlockSpec((2 * TOK, 384), lambda i: (0, 0)),
            pl.BlockSpec((2 * TOK, 384), lambda i: (0, 0)),
            pl.BlockSpec((256, tile), lambda i: (0, i)),
        ],
        out_specs=pl.BlockSpec((8, 32, tile), lambda i: (0, 0, i)),
        compiler_params=params(),
        cost_estimate=pl.CostEstimate(flops=1 << 29, bytes_accessed=4 << 20, transcendentals=0),
    )(where, mine, far, w_out)


def sum_kernel(x_ref, clean_ref, noisy_ref):
    total = x_ref[0].astype(jnp.float32)
    for t in range(1, 8):
        total = total + x_ref[t].astype(jnp.float32)
    clean_ref[...] = total[:16].astype(jnp.bfloat16)
    noisy_ref[...] = total[16:].astype(jnp.bfloat16)


def sum_terms(x):
    tile = 1024
    shape = jax.ShapeDtypeStruct((16, D), jnp.bfloat16)
    return pl.pallas_call(
        sum_kernel,
        grid=(D // tile,),
        out_shape=(shape, shape),
        in_specs=[pl.BlockSpec((8, 32, tile), lambda i: (0, 0, i))],
        out_specs=(pl.BlockSpec((16, tile), lambda i: (0, i)),) * 2,
        compiler_params=params(),
        cost_estimate=pl.CostEstimate(flops=1 << 20, bytes_accessed=2 << 20, transcendentals=0),
    )(x)


def ctx_perm(move):
    pairs = []
    for y in range(2):
        for z in range(NZ):
            for c in range(2):
                target = move(y, z, c)
                if target is not None:
                    ty, tz, tc = target
                    pairs.append((y * 16 + z * 2 + c, ty * 16 + tz * 2 + tc))
    return pairs


CORE_SWAP = ctx_perm(lambda y, z, c: (y, z, 1 - c))
DOWN = ctx_perm(lambda y, z, c: (0, z, c) if y == 1 else None)
UP = ctx_perm(lambda y, z, c: (1, z, c) if y == 0 else None)


def tables(positions):
    half = HEAD_DIM // 2
    freqs = ROPE_BASE ** (-2.0 * jnp.arange(half).astype(jnp.float32) / HEAD_DIM)
    angles = positions.astype(jnp.float32)[:, None] * freqs[None, :]
    cosine, sine = jnp.cos(angles), jnp.sin(angles)
    return jnp.concatenate([cosine, cosine], 1), jnp.concatenate([-sine, sine], 1)


def local(tokens, flags, mask_embed, gain, wq, wk, wv, w_out, block_mask):
    ctx = lax.axis_index("ctx")
    where = jnp.stack([ctx // 16, (ctx // 2) % NZ, ctx % 2]).astype(jnp.int32)
    cosine, sine = tables(ctx * TOK + jnp.arange(TOK, dtype=jnp.int32))
    blocks = jnp.arange(block_mask.shape[0], dtype=jnp.int32)
    table = jnp.stack(
        [
            blocks + 1 - jnp.sum(block_mask % 2, axis=1),
            blocks - jnp.sum(block_mask // 2, axis=1),
        ]
    ).astype(jnp.int32)

    rows, mask_row = norm(tokens, flags, mask_embed, gain)
    gathered = lax.all_to_all(rows, "tp", 0, 0)
    q, kv, kvn = project(gathered, mask_row, wq, wk, wv, cosine, sine)

    pieces = [kv]
    for s in range(1, NZ):
        pieces.append(lax.ppermute(kv, "ctx", ctx_perm(lambda y, z, c: (y, (z + s) % NZ, c))))
    q_other = lax.ppermute(q, "ctx", CORE_SWAP)
    q_far = lax.ppermute(q, "ctx", DOWN)
    q_far_other = lax.ppermute(q_far, "ctx", CORE_SWAP)

    parts = attend(where, table, (q, q_other, q_far, q_far_other), pieces, kvn)
    swapped = lax.ppermute(jnp.stack([parts[1], parts[3]]), "ctx", CORE_SWAP)
    mine, far = merge_cores(parts, swapped)
    far = lax.ppermute(far, "ctx", UP)
    terms = output(where, mine, far, w_out)
    terms = lax.all_to_all(terms, "tp", 0, 0)
    return sum_terms(terms)


def solution(mesh):
    return jax.shard_map(
        local,
        mesh=mesh,
        in_specs=(
            P(("ctx", "tp"), None),
            P(("ctx", "tp")),
            P(),
            P(),
            P(None, "tp"),
            P(None, "tp"),
            P(None, "tp"),
            P("tp", None),
            P(),
        ),
        out_specs=(P(("ctx", "tp"), None), P(("ctx", "tp"), None)),
        check_vma=False,
    )
```

```python
import jax
import jax.numpy as jnp
from jax import lax
from jax.experimental import pallas as pl
from jax.experimental.pallas import tpu as pltpu
from jax.sharding import PartitionSpec as P


HEAD_DIM = 128
BLOCK = 32
ROPE_BASE = 500000.0
EPSILON = 1e-05
TOK = 128
D = 4096
NZ = 8
NT = 8
LOG2E = 1.4426950408889634
SCALE2 = HEAD_DIM ** (-0.5) * LOG2E
HIDDEN = -1e30
FLOOR = -1e29
TERMS_PP = False


VMEM = pl.BlockSpec(memory_space=pltpu.VMEM)
ANY = pl.BlockSpec(memory_space=pl.ANY)
HBM = pl.BlockSpec(memory_space=pltpu.HBM)
SMEM = pl.BlockSpec(memory_space=pltpu.SMEM)


def params(mib=16):
    return pltpu.CompilerParams(vmem_limit_bytes=mib << 20)


def cost(mib, flops=1 << 20):
    return pl.CostEstimate(flops=flops, bytes_accessed=mib << 20, transcendentals=0)


def struct(*shape, dtype=jnp.bfloat16):
    return jax.ShapeDtypeStruct(shape, dtype)


def head(h):
    return slice(h * HEAD_DIM, (h + 1) * HEAD_DIM)


def relative(me, r):
    return ((me // 4) ^ (r // 4)) * 4 + (me + r) % 4


def norm_kernel(tok_hbm, flag_hbm, mask_hbm, gain_hbm, out_ref, mask_out_ref, tok, flag, mask, gain, sems):
    copies = [
        pltpu.make_async_copy(src, dst, sems.at[i])
        for i, (src, dst) in enumerate(
            ((tok_hbm, tok), (flag_hbm, flag), (mask_hbm, mask), (gain_hbm, gain))
        )
    ]
    for copy in copies:
        copy.start()
    for copy in copies:
        copy.wait()
    wide_gain = gain[...].astype(jnp.float32)
    row = lax.broadcasted_iota(jnp.int32, (16, 128), 0)
    flags = jnp.zeros((16, 128), jnp.float32)
    for i in range(16):
        flags = jnp.where(row == i, flag[i].astype(jnp.float32), flags)
    out_ref[:, D:] = flags.astype(jnp.bfloat16)
    wide = tok[...].astype(jnp.float32)
    factor = lax.rsqrt(jnp.mean(wide * wide, axis=-1, keepdims=True) + EPSILON)
    wide_mask = mask[...].astype(jnp.float32)
    square = jnp.sum(wide_mask * wide_mask, axis=0, keepdims=True)
    factor_mask = lax.rsqrt(jnp.sum(square, axis=1, keepdims=True) / D + EPSILON)
    mask_row = wide_mask * factor_mask * wide_gain
    for j in range(D // 128):
        lanes = slice(j * 128, (j + 1) * 128)
        out_ref[:, lanes] = (wide[:, lanes] * factor * wide_gain[j : j + 1]).astype(jnp.bfloat16)
        mask_out_ref[:, lanes] = jnp.broadcast_to(mask_row[j : j + 1], (16, 128)).astype(jnp.bfloat16)


def norm(tokens, flags, mask_embed, gain):
    return pl.pallas_call(
        norm_kernel,
        out_shape=(struct(16, D + 128), struct(16, D)),
        in_specs=[HBM] * 4,
        out_specs=(VMEM, VMEM),
        scratch_shapes=[
            pltpu.VMEM((16, D), jnp.bfloat16),
            pltpu.SMEM((16,), jnp.int32),
            pltpu.VMEM((D // 128, 128), jnp.bfloat16),
            pltpu.VMEM((D // 128, 128), jnp.bfloat16),
            pltpu.SemaphoreType.DMA((4,)),
        ],
        compiler_params=params(),
        cost_estimate=cost(1),
        name="norm",
    )(tokens, flags, mask_embed.reshape(D // 128, 128), gain.reshape(D // 128, 128))


def weights_kernel(mask_ref, wq_hbm, wk_hbm, wv_hbm, w_ref, masked_ref, sems):
    parts = 4
    depth = D // parts
    copies = []
    for i, src in enumerate((wk_hbm, wv_hbm, wq_hbm)):
        for p in range(parts):
            rows = pl.ds(p * depth, depth)
            copies.append(
                pltpu.make_async_copy(src.at[rows, :], w_ref.at[rows, pl.ds(i * 256, 256)], sems.at[i, p])
            )
    for copy in copies:
        copy.start()
    for copy in copies:
        copy.wait()
    for i in range(3):
        masked_ref[:, i * 256 : (i + 1) * 256] = jnp.dot(
            mask_ref[...], w_ref[:, i * 256 : (i + 1) * 256], preferred_element_type=jnp.float32
        )[:8]


def load_weights(mask_row, wq, wk, wv):
    return pl.pallas_call(
        weights_kernel,
        out_shape=(struct(D, 768), struct(8, 768, dtype=jnp.float32)),
        in_specs=[VMEM, HBM, HBM, HBM],
        out_specs=(VMEM, VMEM),
        scratch_shapes=[pltpu.SemaphoreType.DMA((3, 4))],
        compiler_params=params(),
        cost_estimate=cost(12),
        name="weights",
    )(mask_row, wq, wk, wv)


def place():
    ctx = lax.axis_index("ctx")
    return ctx // 16, (ctx // 2) % NZ, ctx % 2


def rotary(v, cosine, sine):
    return v * cosine + pltpu.roll(v, HEAD_DIM // 2, 1) * sine


def both(rows_ref, w_ref, masked_ref, i):
    cols = slice(i * 256, (i + 1) * 256)
    noisy = rows_ref[:, D : D + 1].astype(jnp.float32) > 0.5
    clean = jnp.dot(rows_ref[:, :D], w_ref[:, cols], preferred_element_type=jnp.float32)
    return clean, jnp.where(noisy, masked_ref[0:1, cols], clean)


def key_kernel(*refs):
    g_refs = refs[:NT]
    w_ref, masked_ref, cos_ref, sin_ref, kv_ref, kvn_ref, rows_ref = refs[NT:]
    me = lax.axis_index("tp")
    for r in range(NT):
        rows_ref[pl.ds(pl.multiple_of(relative(me, r) * 16, 16), 16), :] = g_refs[r][...]
    cosine, sine = cos_ref[...], sin_ref[...]
    keys = both(rows_ref, w_ref, masked_ref, 0)
    values = both(rows_ref, w_ref, masked_ref, 1)
    for h in range(2):
        for k, v, ref in zip(keys, values, (kv_ref, kvn_ref)):
            ref[:, head(h)] = rotary(k[:, head(h)], cosine, sine).astype(jnp.bfloat16)
            ref[:, head(2 + h)] = v[:, head(h)].astype(jnp.bfloat16)


def project_keys(gathered, w, masked, cosine, sine):
    return pl.pallas_call(
        key_kernel,
        out_shape=(struct(TOK, 512), struct(TOK, 512), struct(TOK, D + 128)),
        in_specs=[VMEM] * (NT + 4),
        out_specs=(VMEM,) * 3,
        compiler_params=params(),
        cost_estimate=cost(6, 1 << 30),
        name="keys",
    )(*gathered, w, masked, cosine, sine)


def query_kernel(rows_ref, w_ref, masked_ref, cos_ref, sin_ref, q_ref):
    cosine, sine = cos_ref[...], sin_ref[...]
    for i, q in enumerate(both(rows_ref, w_ref, masked_ref, 2)):
        for h in range(2):
            q_ref[i * TOK : (i + 1) * TOK, head(h)] = rotary(q[:, head(h)], cosine, sine).astype(jnp.bfloat16)


def project_queries(rows, w, masked, cosine, sine):
    return pl.pallas_call(
        query_kernel,
        out_shape=struct(2 * TOK, 256),
        in_specs=[VMEM] * 5,
        out_specs=VMEM,
        compiler_params=params(),
        cost_estimate=cost(3, 1 << 29),
        name="queries",
    )(rows, w, masked, cosine, sine)


def pack_stats(lses):
    rows = lses[0].shape[0]
    lane = lax.broadcasted_iota(jnp.int32, (rows, 128), 1)
    total = jnp.zeros((rows, 128), jnp.float32)
    for h, lse in enumerate(lses):
        rest = lse
        for part in range(3):
            piece = rest.astype(jnp.bfloat16).astype(jnp.float32)
            total = jnp.where(lane == h * 4 + part, piece, total)
            rest = rest - piece
    return total.astype(jnp.bfloat16)


def unpack_stats(block):
    wide = block.astype(jnp.float32)
    return [
        wide[:, h * 4 : h * 4 + 1] + wide[:, h * 4 + 1 : h * 4 + 2] + wide[:, h * 4 + 2 : h * 4 + 3]
        for h in range(2)
    ]


def attend_kernel(far, *refs):
    table_ref, mine_ref, other_ref = refs[:3]
    kv_refs = refs[3 : 3 + NZ]
    rest = refs[3 + NZ :]
    kvn_ref = None if far else rest[0]
    out_mine, out_other, keys = rest[-3:]
    y, z, c = place()
    col = lax.broadcasted_iota(jnp.int32, (1, NZ * TOK), 1)

    def work():
        for s in range(NZ):
            keys[s * TOK : (s + 1) * TOK, :] = kv_refs[s][...]
        source = (z - col // TOK) & (NZ - 1)
        key_block = (y * 16 + source * 2 + c) * 4 + (col % TOK) // BLOCK
        part = lax.broadcasted_iota(jnp.int32, (2 * TOK, 1), 0) // BLOCK
        for g, q_ref, out_ref in ((1, other_ref, out_other), (0, mine_ref, out_mine)):
            yq = 1 if far else y
            cq = c if g == 0 else 1 - c
            first = (yq * 16 + z * 2 + cq) * 4
            low = jnp.zeros((2 * TOK, 1), jnp.int32)
            high = jnp.zeros((2 * TOK, 1), jnp.int32)
            for p in range(8):
                copy, block = p // 4, first + p % 4
                low = jnp.where(part == p, table_ref[copy, block], low)
                high = jnp.where(part == p, block - copy, high)
            visible = (key_block >= low) & (key_block <= high)
            lses = []
            for h in range(2):
                q = q_ref[:, head(h)]
                scores = lax.dot_general(
                    q, keys[:, head(h)], (((1,), (1,)), ((), ())), preferred_element_type=jnp.float32
                ) * SCALE2
                scores = jnp.where(visible, scores, HIDDEN)
                peak = jnp.maximum(jnp.max(scores, axis=-1, keepdims=True), FLOOR)
                near_part = g == 0 and not far
                if near_part:
                    own = lax.dot_general(
                        q[TOK:], kvn_ref[:, head(h)], (((1,), (1,)), ((), ())),
                        preferred_element_type=jnp.float32,
                    ) * SCALE2
                    near = (
                        lax.broadcasted_iota(jnp.int32, (TOK, TOK), 0) // BLOCK
                        == lax.broadcasted_iota(jnp.int32, (TOK, TOK), 1) // BLOCK
                    )
                    own = jnp.where(near, own, HIDDEN)
                    peak_own = jnp.maximum(peak[TOK:], jnp.max(own, axis=-1, keepdims=True))
                    peak = jnp.concatenate([peak[:TOK], peak_own], axis=0)
                weights = jnp.exp2(scores - peak)
                total = jnp.sum(weights, axis=-1, keepdims=True)
                weighted = jnp.dot(
                    weights.astype(jnp.bfloat16), keys[:, head(2 + h)], preferred_element_type=jnp.float32
                )
                if near_part:
                    wown = jnp.exp2(own - peak_own)
                    total = total + jnp.concatenate(
                        [jnp.zeros((TOK, 1), jnp.float32), jnp.sum(wown, axis=-1, keepdims=True)], axis=0
                    )
                    extra = jnp.dot(
                        wown.astype(jnp.bfloat16), kvn_ref[:, head(2 + h)], preferred_element_type=jnp.float32
                    )
                    weighted = weighted + jnp.concatenate(
                        [jnp.zeros((TOK, HEAD_DIM), jnp.float32), extra], axis=0
                    )
                some = total > 0.0
                safe = jnp.where(some, total, 1.0)
                out_ref[:, head(h)] = (weighted / safe).astype(jnp.bfloat16)
                lses.append(jnp.where(some, peak + jnp.log2(safe), FLOOR))
            out_ref[:, 256:] = pack_stats(lses)

    if far:
        pl.when(y == 0)(work)

        @pl.when(y == 1)
        def _():
            out_mine[...] = jnp.zeros_like(out_mine)
            out_other[...] = jnp.zeros_like(out_other)
    else:
        work()


def attend(table, mine, other, key_values, *extra):
    far = not extra

    def kernel(*refs):
        attend_kernel(far, *refs)

    return pl.pallas_call(
        kernel,
        out_shape=(struct(2 * TOK, 384), struct(2 * TOK, 384)),
        in_specs=[SMEM] + [VMEM] * (2 + NZ) + ([] if far else [VMEM, ANY]),
        out_specs=(VMEM, VMEM),
        scratch_shapes=[pltpu.VMEM((NZ * TOK, 512), jnp.bfloat16)],
        compiler_params=params(),
        cost_estimate=cost(4, 1 << 29),
        name="attend_far" if far else "attend_near",
    )(table, mine, other, *key_values, *extra)


def merge(a, b):
    outs, lses = [], []
    sa, sb = unpack_stats(a[:, 256:]), unpack_stats(b[:, 256:])
    for h in range(2):
        peak = jnp.maximum(sa[h], sb[h])
        wa, wb = jnp.exp2(sa[h] - peak), jnp.exp2(sb[h] - peak)
        total = wa + wb
        mixed = a[:, head(h)].astype(jnp.float32) * wa + b[:, head(h)].astype(jnp.float32) * wb
        outs.append(mixed / total)
        lses.append(peak + jnp.log2(total))
    return outs, lses


def merge_kernel(mine_ref, swap_ref, out_ref):
    outs, lses = merge(mine_ref[...], swap_ref[...])
    for h in range(2):
        out_ref[:, head(h)] = outs[h].astype(jnp.bfloat16)
    out_ref[:, 256:] = pack_stats(lses)


def merge_cores(mine, swapped):
    return pl.pallas_call(
        merge_kernel,
        out_shape=struct(2 * TOK, 384),
        in_specs=[VMEM, VMEM],
        out_specs=VMEM,
        compiler_params=params(),
        cost_estimate=cost(1),
    )(mine, swapped)


def output_kernel(self_ref, far_ref, w_ref, *refs):
    att = refs[-1]
    outs, _ = merge(self_ref[...], far_ref[...])
    upper_line = place()[0] == 1
    for h in range(2):
        alone = self_ref[:, head(h)].astype(jnp.float32)
        value = jnp.where(upper_line, outs[h], alone).astype(jnp.bfloat16)
        for t in range(NT):
            for s in range(2):
                att[t, s * 16 : (s + 1) * 16, head(h)] = value[s * TOK + t * 16 : s * TOK + (t + 1) * 16]
    me = lax.axis_index("tp")
    if TERMS_PP:
        rows = jnp.concatenate([att[relative(me, r)] for r in range(NT)], axis=0)
    else:
        rows = att[...].reshape(2 * TOK, 256)
    for i in range(8):
        cols = slice(i * 512, (i + 1) * 512)
        terms = jnp.dot(rows, w_ref[:, cols], preferred_element_type=jnp.float32).astype(jnp.bfloat16)
        if TERMS_PP:
            for r in range(NT):
                refs[r][:, cols] = terms[r * 32 : (r + 1) * 32]
        else:
            refs[0][:, :, cols] = terms.reshape(NT, 32, 512)


def output(mine, far, w_out):
    shapes = (struct(32, D),) * NT if TERMS_PP else (struct(NT, 32, D),)
    return pl.pallas_call(
        output_kernel,
        out_shape=shapes,
        in_specs=[VMEM, VMEM, VMEM],
        out_specs=(VMEM,) * len(shapes),
        scratch_shapes=[pltpu.VMEM((NT, 32, 256), jnp.bfloat16)],
        compiler_params=params(),
        cost_estimate=cost(4, 1 << 29),
        name="terms",
    )(mine, far, w_out)


def sum_kernel(*refs):
    clean_ref, noisy_ref = refs[-2:]
    blocks = refs[:-2]
    total = 0.0
    for t in range(NT):
        block = blocks[t][...] if TERMS_PP else blocks[0][t]
        total = total + block.astype(jnp.float32)
    clean_ref[...] = total[:16].astype(jnp.bfloat16)
    noisy_ref[...] = total[16:].astype(jnp.bfloat16)


def sum_terms(blocks):
    tile = 1024
    if TERMS_PP:
        specs = [pl.BlockSpec((32, tile), lambda i: (0, i))] * NT
    else:
        specs = [pl.BlockSpec((NT, 32, tile), lambda i: (0, 0, i))]
    return pl.pallas_call(
        sum_kernel,
        grid=(D // tile,),
        out_shape=(struct(16, D), struct(16, D)),
        in_specs=specs,
        out_specs=(pl.BlockSpec((16, tile), lambda i: (0, i)),) * 2,
        compiler_params=params(),
        cost_estimate=cost(2),
    )(*blocks)


def ctx_perm(move):
    pairs = []
    for y in range(2):
        for z in range(NZ):
            for c in range(2):
                target = move(y, z, c)
                if target is not None:
                    ty, tz, tc = target
                    pairs.append((y * 16 + z * 2 + c, ty * 16 + tz * 2 + tc))
    return pairs


def ctx_move(x, move):
    return lax.ppermute(x, "ctx", ctx_perm(move))


def swap(x):
    return ctx_move(x, lambda y, z, c: (y, z, 1 - c))


def tp_move(x, r):
    return lax.ppermute(x, "tp", [(i, relative(i, r)) for i in range(NT)])


def tables(positions):
    half = HEAD_DIM // 2
    freqs = ROPE_BASE ** (-2.0 * jnp.arange(half).astype(jnp.float32) / HEAD_DIM)
    angles = positions.astype(jnp.float32)[:, None] * freqs[None, :]
    cosine, sine = jnp.cos(angles), jnp.sin(angles)
    return jnp.concatenate([cosine, cosine], 1), jnp.concatenate([-sine, sine], 1)


def layer(tokens, flags, mask_embed, gain, wq, wk, wv, w_out, block_mask):
    ctx = lax.axis_index("ctx")
    cosine, sine = tables(ctx * TOK + jnp.arange(TOK, dtype=jnp.int32))
    blocks = jnp.arange(block_mask.shape[0], dtype=jnp.int32)
    table = jnp.stack(
        [
            blocks + 1 - jnp.sum(block_mask % 2, axis=1),
            blocks - jnp.sum(block_mask // 2, axis=1),
        ]
    ).astype(jnp.int32)

    rows, mask_row = norm(tokens, flags, mask_embed, gain)
    partner = tp_move(rows, 4)
    gathered = [rows] + [tp_move(rows, 4 - r) for r in (1, 2, 3)]
    gathered += [partner] + [tp_move(partner, 4 - r) for r in (1, 2, 3)]
    w, masked = load_weights(mask_row, wq, wk, wv)
    kv, kvn, all_rows = project_keys(gathered, w, masked, cosine, sine)

    pieces = [kv]
    for s in range(1, NZ):
        pieces.append(ctx_move(kv, lambda y, z, c: (y, (z + s) % NZ, c)))
    q = project_queries(all_rows, w, masked, cosine, sine)
    q_far = ctx_move(q, lambda y, z, c: (0, z, c) if y == 1 else None)
    q_other = swap(q)
    q_far_other = swap(q_far)

    far, far_other = attend(table, q_far, q_far_other, pieces)
    far = merge_cores(far, swap(far_other))
    returned = ctx_move(far, lambda y, z, c: (1, z, c) if y == 0 else None)
    mine, other = attend(table, q, q_other, pieces, kvn, far)
    mine = merge_cores(mine, swap(other))
    terms = list(output(mine, returned, w_out))
    if TERMS_PP:
        for r in range(1, NT):
            terms[r] = tp_move(terms[r], r)
    else:
        terms = [lax.all_to_all(terms[0], "tp", 0, 0)]
    return sum_terms(terms)


def solution(mesh):
    return jax.shard_map(
        layer,
        mesh=mesh,
        in_specs=(
            P(("ctx", "tp"), None),
            P(("ctx", "tp")),
            P(),
            P(),
            P(None, "tp"),
            P(None, "tp"),
            P(None, "tp"),
            P("tp", None),
            P(),
        ),
        out_specs=(P(("ctx", "tp"), None), P(("ctx", "tp"), None)),
        check_vma=False,
    )
```

```python
import jax
import jax.numpy as jnp
from jax import lax
from jax.experimental import pallas as pl
from jax.experimental.pallas import tpu as pltpu
from jax.sharding import PartitionSpec as P


HEAD_DIM = 128
BLOCK = 32
ROPE_BASE = 500000.0
EPSILON = 1e-05
TOK = 128
D = 4096
NZ = 8
NT = 8
LOG2E = 1.4426950408889634
SCALE2 = HEAD_DIM ** (-0.5) * LOG2E
HIDDEN = -1e30
FLOOR = -1e29
TERMS_PP = True


VMEM = pl.BlockSpec(memory_space=pltpu.VMEM)
ANY = pl.BlockSpec(memory_space=pl.ANY)
HBM = pl.BlockSpec(memory_space=pltpu.HBM)
SMEM = pl.BlockSpec(memory_space=pltpu.SMEM)


def params(mib=16):
    return pltpu.CompilerParams(vmem_limit_bytes=mib << 20)


def cost(mib, flops=1 << 20):
    return pl.CostEstimate(flops=flops, bytes_accessed=mib << 20, transcendentals=0)


def struct(*shape, dtype=jnp.bfloat16):
    return jax.ShapeDtypeStruct(shape, dtype)


def head(h):
    return slice(h * HEAD_DIM, (h + 1) * HEAD_DIM)


def relative(me, r):
    return ((me // 4) ^ (r // 4)) * 4 + (me + r) % 4


def norm_kernel(tok_hbm, flag_hbm, mask_hbm, gain_hbm, out_ref, mask_out_ref, tok, flag, mask, gain, sems):
    copies = [
        pltpu.make_async_copy(src, dst, sems.at[i])
        for i, (src, dst) in enumerate(
            ((tok_hbm, tok), (flag_hbm, flag), (mask_hbm, mask), (gain_hbm, gain))
        )
    ]
    for copy in copies:
        copy.start()
    for copy in copies:
        copy.wait()
    wide_gain = gain[...].astype(jnp.float32)
    row = lax.broadcasted_iota(jnp.int32, (16, 128), 0)
    flags = jnp.zeros((16, 128), jnp.float32)
    for i in range(16):
        flags = jnp.where(row == i, flag[i].astype(jnp.float32), flags)
    out_ref[:, D:] = flags.astype(jnp.bfloat16)
    wide = tok[...].astype(jnp.float32)
    factor = lax.rsqrt(jnp.mean(wide * wide, axis=-1, keepdims=True) + EPSILON)
    wide_mask = mask[...].astype(jnp.float32)
    square = jnp.sum(wide_mask * wide_mask, axis=0, keepdims=True)
    factor_mask = lax.rsqrt(jnp.sum(square, axis=1, keepdims=True) / D + EPSILON)
    mask_row = wide_mask * factor_mask * wide_gain
    for j in range(D // 128):
        lanes = slice(j * 128, (j + 1) * 128)
        out_ref[:, lanes] = (wide[:, lanes] * factor * wide_gain[j : j + 1]).astype(jnp.bfloat16)
        mask_out_ref[:, lanes] = jnp.broadcast_to(mask_row[j : j + 1], (16, 128)).astype(jnp.bfloat16)


def norm(tokens, flags, mask_embed, gain):
    return pl.pallas_call(
        norm_kernel,
        out_shape=(struct(16, D + 128), struct(16, D)),
        in_specs=[HBM] * 4,
        out_specs=(VMEM, VMEM),
        scratch_shapes=[
            pltpu.VMEM((16, D), jnp.bfloat16),
            pltpu.SMEM((16,), jnp.int32),
            pltpu.VMEM((D // 128, 128), jnp.bfloat16),
            pltpu.VMEM((D // 128, 128), jnp.bfloat16),
            pltpu.SemaphoreType.DMA((4,)),
        ],
        compiler_params=pltpu.CompilerParams(vmem_limit_bytes=16 << 20),
        cost_estimate=cost(1),
        name="norm",
    )(*(pltpu.with_memory_space_constraint(v, pltpu.HBM) for v in (tokens, flags, mask_embed.reshape(D // 128, 128), gain.reshape(D // 128, 128))))


def weights_kernel(mask_ref, wq_hbm, wk_hbm, wv_hbm, w_ref, masked_ref, sems):
    parts = 4
    depth = D // parts
    copies = []
    for i, src in enumerate((wk_hbm, wv_hbm, wq_hbm)):
        for p in range(parts):
            rows = pl.ds(p * depth, depth)
            copies.append(
                pltpu.make_async_copy(src.at[rows, :], w_ref.at[rows, pl.ds(i * 256, 256)], sems.at[i, p])
            )
    for copy in copies:
        copy.start()
    for copy in copies:
        copy.wait()
    for i in range(3):
        masked_ref[:, i * 256 : (i + 1) * 256] = jnp.dot(
            mask_ref[...], w_ref[:, i * 256 : (i + 1) * 256], preferred_element_type=jnp.float32
        )[:8]


def load_weights(mask_row, wq, wk, wv):
    return pl.pallas_call(
        weights_kernel,
        out_shape=(struct(D, 768), struct(8, 768, dtype=jnp.float32)),
        in_specs=[VMEM, HBM, HBM, HBM],
        out_specs=(VMEM, VMEM),
        scratch_shapes=[pltpu.SemaphoreType.DMA((3, 4))],
        compiler_params=pltpu.CompilerParams(vmem_limit_bytes=16 << 20),
        cost_estimate=cost(12),
        name="weights",
    )(mask_row, *(pltpu.with_memory_space_constraint(w, pltpu.HBM) for w in (wq, wk, wv)))


def place():
    ctx = lax.axis_index("ctx")
    return ctx // 16, (ctx // 2) % NZ, ctx % 2


def rotary(v, cosine, sine):
    return v * cosine + pltpu.roll(v, HEAD_DIM // 2, 1) * sine


def both(rows_ref, w_ref, masked_ref, i):
    cols = slice(i * 256, (i + 1) * 256)
    noisy = rows_ref[:, D : D + 1].astype(jnp.float32) > 0.5
    clean = jnp.dot(rows_ref[:, :D], w_ref[:, cols], preferred_element_type=jnp.float32)
    return clean, jnp.where(noisy, masked_ref[0:1, cols], clean)


def key_kernel(*refs):
    g_refs = refs[:NT]
    w_ref, masked_ref, cos_ref, sin_ref, kv_ref, kvn_ref, rows_ref = refs[NT:]
    me = lax.axis_index("tp")
    for r in range(NT):
        rows_ref[pl.ds(pl.multiple_of(relative(me, r) * 16, 16), 16), :] = g_refs[r][...]
    cosine, sine = cos_ref[...], sin_ref[...]
    keys = both(rows_ref, w_ref, masked_ref, 0)
    values = both(rows_ref, w_ref, masked_ref, 1)
    for h in range(2):
        for k, v, ref in zip(keys, values, (kv_ref, kvn_ref)):
            ref[:, head(h)] = rotary(k[:, head(h)], cosine, sine).astype(jnp.bfloat16)
            ref[:, head(2 + h)] = v[:, head(h)].astype(jnp.bfloat16)


def project_keys(gathered, w, masked, cosine, sine):
    return pl.pallas_call(
        key_kernel,
        out_shape=(struct(TOK, 512), struct(TOK, 512), struct(TOK, D + 128)),
        in_specs=[VMEM] * (NT + 4),
        out_specs=(VMEM,) * 3,
        compiler_params=params(),
        cost_estimate=cost(6, 1 << 30),
        name="keys",
    )(*gathered, w, masked, cosine, sine)


def query_kernel(rows_ref, w_ref, masked_ref, cos_ref, sin_ref, q_ref):
    cosine, sine = cos_ref[...], sin_ref[...]
    for i, q in enumerate(both(rows_ref, w_ref, masked_ref, 2)):
        for h in range(2):
            q_ref[i * TOK : (i + 1) * TOK, head(h)] = rotary(q[:, head(h)], cosine, sine).astype(jnp.bfloat16)


def project_queries(rows, w, masked, cosine, sine):
    return pl.pallas_call(
        query_kernel,
        out_shape=struct(2 * TOK, 256),
        in_specs=[VMEM] * 5,
        out_specs=VMEM,
        compiler_params=params(),
        cost_estimate=cost(3, 1 << 29),
        name="queries",
    )(rows, w, masked, cosine, sine)


def pack_stats(lses):
    rows = lses[0].shape[0]
    lane = lax.broadcasted_iota(jnp.int32, (rows, 128), 1)
    total = jnp.zeros((rows, 128), jnp.float32)
    for h, lse in enumerate(lses):
        rest = lse
        for part in range(3):
            piece = rest.astype(jnp.bfloat16).astype(jnp.float32)
            total = jnp.where(lane == h * 4 + part, piece, total)
            rest = rest - piece
    return total.astype(jnp.bfloat16)


def unpack_stats(block):
    wide = block.astype(jnp.float32)
    return [
        wide[:, h * 4 : h * 4 + 1] + wide[:, h * 4 + 1 : h * 4 + 2] + wide[:, h * 4 + 2 : h * 4 + 3]
        for h in range(2)
    ]


def unpack(ref):
    block = ref[...]
    return [block[:, head(h)].astype(jnp.float32) for h in range(2)], unpack_stats(block[:, 256:])


def pack(part, ref):
    outs, lses = part
    for h in range(2):
        ref[:, head(h)] = outs[h].astype(jnp.bfloat16)
    ref[:, 256:] = pack_stats(lses)


def merge(a, b):
    outs, lses = [], []
    for h in range(2):
        peak = jnp.maximum(a[1][h], b[1][h])
        wa, wb = jnp.exp2(a[1][h] - peak), jnp.exp2(b[1][h] - peak)
        total = wa + wb
        outs.append((a[0][h] * wa + b[0][h] * wb) / total)
        lses.append(peak + jnp.log2(total))
    return outs, lses


TILES = ((0, 0), (2, 0), (2, 1), (1, 0), (1, 1), (3, 0), (3, 1), (4, 0))
EARLY = TILES[:5]
LATE = TILES[5:]


def tile_block(tile, y, z, c):
    step, flip = tile
    source = (z + jnp.where(c == 0, NZ - step, step)) % NZ
    core = 1 - c if flip else c
    return (y * 16 + source * 2 + core) * 4


def partial(q, keys, tiles, table_ref, yq, cq, near=None):
    y, z, c = place()
    col = lax.broadcasted_iota(jnp.int32, (1, len(tiles) * TOK), 1)
    key_block = (col % TOK) // BLOCK
    for i, tile in enumerate(tiles):
        key_block = jnp.where(col // TOK == i, key_block + tile_block(tile, y, z, c), key_block)
    part = lax.broadcasted_iota(jnp.int32, (2 * TOK, 1), 0) // BLOCK
    first = (yq * 16 + z * 2 + cq) * 4
    low = jnp.zeros((2 * TOK, 1), jnp.int32)
    high = jnp.zeros((2 * TOK, 1), jnp.int32)
    for p in range(8):
        copy, block = p // 4, first + p % 4
        low = jnp.where(part == p, table_ref[copy, block], low)
        high = jnp.where(part == p, block - copy, high)
    visible = (key_block >= low) & (key_block <= high)
    outs, lses = [], []
    for h in range(2):
        qh = q[:, head(h)]
        scores = lax.dot_general(
            qh, keys[:, head(h)], (((1,), (1,)), ((), ())), preferred_element_type=jnp.float32
        ) * SCALE2
        scores = jnp.where(visible, scores, HIDDEN)
        peak = jnp.maximum(jnp.max(scores, axis=-1, keepdims=True), FLOOR)
        if near is not None:
            kvn_ref, wanted = near
            own = lax.dot_general(
                qh[TOK:], kvn_ref[:, head(h)], (((1,), (1,)), ((), ())), preferred_element_type=jnp.float32
            ) * SCALE2
            same = (
                lax.broadcasted_iota(jnp.int32, (TOK, TOK), 0) // BLOCK
                == lax.broadcasted_iota(jnp.int32, (TOK, TOK), 1) // BLOCK
            ) & wanted
            own = jnp.where(same, own, HIDDEN)
            peak_own = jnp.maximum(peak[TOK:], jnp.max(own, axis=-1, keepdims=True))
            peak = jnp.concatenate([peak[:TOK], peak_own], axis=0)
        weights = jnp.exp2(scores - peak)
        total = jnp.sum(weights, axis=-1, keepdims=True)
        weighted = jnp.dot(
            weights.astype(jnp.bfloat16), keys[:, head(2 + h)], preferred_element_type=jnp.float32
        )
        if near is not None:
            wown = jnp.exp2(own - peak_own)
            total = total + jnp.concatenate(
                [jnp.zeros((TOK, 1), jnp.float32), jnp.sum(wown, axis=-1, keepdims=True)], axis=0
            )
            extra = jnp.dot(
                wown.astype(jnp.bfloat16), kvn_ref[:, head(2 + h)], preferred_element_type=jnp.float32
            )
            weighted = weighted + jnp.concatenate(
                [jnp.zeros((TOK, HEAD_DIM), jnp.float32), extra], axis=0
            )
        some = total > 0.0
        safe = jnp.where(some, total, 1.0)
        outs.append(weighted / safe)
        lses.append(jnp.where(some, peak + jnp.log2(safe), FLOOR))
    return outs, lses


def save(part, ref):
    outs, lses = part
    for h in range(2):
        ref[:, head(h)] = outs[h]
        ref[:, head(2 + h)] = jnp.broadcast_to(lses[h], (2 * TOK, HEAD_DIM))


def saved(ref):
    return [ref[:, head(h)] for h in range(2)], [ref[:, (2 + h) * 128 : (2 + h) * 128 + 1] for h in range(2)]


def early_kernel(table_ref, q_ref, other_ref, far_ref, far_other_ref, own_ref, two_ref, one_ref, kvn_ref,
                 up_mine, up_other, low_mine, low_other, keys):
    y, _, c = place()
    keys[:TOK] = own_ref[0]
    keys[TOK : 3 * TOK] = two_ref[...].reshape(2 * TOK, 512)
    keys[3 * TOK :] = one_ref[...].reshape(2 * TOK, 512)
    tiles = EARLY
    mine = jnp.where(y == 1, q_ref[...], far_ref[...])
    other = jnp.where(y == 1, other_ref[...], far_other_ref[...])
    save(partial(mine, keys, tiles, table_ref, 1, c, (kvn_ref, y == 1)), up_mine)
    save(partial(other, keys, tiles, table_ref, 1, 1 - c), up_other)

    @pl.when(y == 0)
    def _():
        save(partial(q_ref[...], keys, tiles, table_ref, 0, c, (kvn_ref, y == 0)), low_mine)
        save(partial(other_ref[...], keys, tiles, table_ref, 0, 1 - c), low_other)

    @pl.when(y == 1)
    def _():
        low_mine[...] = jnp.zeros_like(low_mine)
        low_other[...] = jnp.zeros_like(low_other)


def early(table, q, other, far, far_other, own, two, one, kvn):
    return pl.pallas_call(
        early_kernel,
        out_shape=(struct(2 * TOK, 512, dtype=jnp.float32),) * 4,
        in_specs=[SMEM] + [VMEM] * 8,
        out_specs=(VMEM,) * 4,
        scratch_shapes=[pltpu.VMEM((len(EARLY) * TOK, 512), jnp.bfloat16)],
        compiler_params=params(),
        cost_estimate=cost(4, 1 << 29),
        name="early",
    )(table, q, other, far, far_other, own, two, one, kvn)


def late_kernel(line, table_ref, q_ref, other_ref, far_ref, far_other_ref, three_ref, half_ref, mine_ref, swap_ref, _,
                out_mine, out_other, keys):
    y, _, c = place()

    def work():
        keys[: 2 * TOK] = three_ref[...].reshape(2 * TOK, 512)
        keys[2 * TOK :] = half_ref[...]
        tiles = LATE
        if line == 1:
            mine = jnp.where(y == 1, q_ref[...], far_ref[...])
            other = jnp.where(y == 1, other_ref[...], far_other_ref[...])
        else:
            mine, other = q_ref[...], other_ref[...]
        pack(merge(saved(swap_ref), partial(other, keys, tiles, table_ref, line, 1 - c)), out_other)
        pack(merge(saved(mine_ref), partial(mine, keys, tiles, table_ref, line, c)), out_mine)

    if line == 1:
        work()
    else:
        pl.when(y == 0)(work)

        @pl.when(y == 1)
        def _():
            out_mine[...] = jnp.zeros_like(out_mine)
            out_other[...] = jnp.zeros_like(out_other)


def late(line, table, q, other, far, far_other, three, half, mine, swapped, after):
    def kernel(*refs):
        late_kernel(line, *refs)

    return pl.pallas_call(
        kernel,
        out_shape=(struct(2 * TOK, 384), struct(2 * TOK, 384)),
        in_specs=[SMEM] + [VMEM] * 8 + [ANY],
        out_specs=(VMEM, VMEM),
        scratch_shapes=[pltpu.VMEM((len(LATE) * TOK, 512), jnp.bfloat16)],
        compiler_params=params(),
        cost_estimate=cost(4, 1 << 29),
        name="late_upper" if line == 1 else "late_lower",
    )(table, q, other, far, far_other, three, half, mine, swapped, after)


def merge_kernel(mine_ref, swap_ref, out_ref):
    pack(merge(unpack(mine_ref), unpack(swap_ref)), out_ref)


def merge_cores(mine, swapped):
    return pl.pallas_call(
        merge_kernel,
        out_shape=struct(2 * TOK, 384),
        in_specs=[VMEM, VMEM],
        out_specs=VMEM,
        compiler_params=params(),
        cost_estimate=cost(1),
        name="merge",
    )(mine, swapped)


def output_kernel(upper_ref, lower_ref, far_ref, w_ref, *refs):
    att = refs[-1]
    outs, _ = merge(unpack(upper_ref), unpack(far_ref))
    upper_line = place()[0] == 1
    lower, _ = unpack(lower_ref)
    for h in range(2):
        value = jnp.where(upper_line, outs[h], lower[h]).astype(jnp.bfloat16)
        for t in range(NT):
            for s in range(2):
                att[t, s * 16 : (s + 1) * 16, head(h)] = value[s * TOK + t * 16 : s * TOK + (t + 1) * 16]
    me = lax.axis_index("tp")
    if TERMS_PP:
        rows = jnp.concatenate([att[relative(me, r)] for r in range(NT)], axis=0)
    else:
        rows = att[...].reshape(2 * TOK, 256)
    for i in range(8):
        cols = slice(i * 512, (i + 1) * 512)
        terms = jnp.dot(rows, w_ref[:, cols], preferred_element_type=jnp.float32).astype(jnp.bfloat16)
        if TERMS_PP:
            for r in range(NT):
                refs[r][:, cols] = terms[r * 32 : (r + 1) * 32]
        else:
            refs[0][:, :, cols] = terms.reshape(NT, 32, 512)


def output(upper, lower, far, w_out):
    shapes = (struct(32, D),) * NT if TERMS_PP else (struct(NT, 32, D),)
    return pl.pallas_call(
        output_kernel,
        out_shape=shapes,
        in_specs=[VMEM] * 4,
        out_specs=(VMEM,) * len(shapes),
        scratch_shapes=[pltpu.VMEM((NT, 32, 256), jnp.bfloat16)],
        compiler_params=params(),
        cost_estimate=cost(4, 1 << 29),
        name="terms",
    )(upper, lower, far, w_out)


def sum_kernel(*refs):
    clean_ref, noisy_ref = refs[-2:]
    blocks = refs[:-2]
    total = 0.0
    for t in range(NT):
        block = blocks[t][...] if TERMS_PP else blocks[0][t]
        total = total + block.astype(jnp.float32)
    clean_ref[...] = total[:16].astype(jnp.bfloat16)
    noisy_ref[...] = total[16:].astype(jnp.bfloat16)


def sum_terms(blocks):
    return pl.pallas_call(
        sum_kernel,
        out_shape=(struct(16, D), struct(16, D)),
        in_specs=[VMEM] * len(blocks),
        out_specs=(VMEM, VMEM),
        compiler_params=params(),
        cost_estimate=cost(2),
        name="sum_terms",
    )(*blocks)


def ctx_perm(move):
    pairs = []
    for y in range(2):
        for z in range(NZ):
            for c in range(2):
                target = move(y, z, c)
                if target is not None:
                    ty, tz, tc = target
                    pairs.append((y * 16 + z * 2 + c, ty * 16 + tz * 2 + tc))
    return pairs


def ctx_move(x, move):
    return lax.ppermute(x, "ctx", ctx_perm(move))


def swap(x):
    return ctx_move(x, lambda y, z, c: (y, z, 1 - c))


def tp_move(x, r):
    return lax.ppermute(x, "tp", [(i, relative(i, r)) for i in range(NT)])


def tables(positions):
    half = HEAD_DIM // 2
    freqs = ROPE_BASE ** (-2.0 * jnp.arange(half).astype(jnp.float32) / HEAD_DIM)
    angles = positions.astype(jnp.float32)[:, None] * freqs[None, :]
    cosine, sine = jnp.cos(angles), jnp.sin(angles)
    return jnp.concatenate([cosine, cosine], 1), jnp.concatenate([-sine, sine], 1)


def layer(tokens, flags, mask_embed, gain, wq, wk, wv, w_out, block_mask):
    ctx = lax.axis_index("ctx")
    cosine, sine = tables(ctx * TOK + jnp.arange(TOK, dtype=jnp.int32))
    blocks = jnp.arange(block_mask.shape[0], dtype=jnp.int32)
    table = jnp.stack(
        [
            blocks + 1 - jnp.sum(block_mask % 2, axis=1),
            blocks - jnp.sum(block_mask // 2, axis=1),
        ]
    ).astype(jnp.int32)

    rows, mask_row = norm(tokens, flags, mask_embed, gain)
    partner = tp_move(rows, 4)
    gathered = [rows] + [tp_move(rows, 4 - r) for r in (1, 2, 3)]
    gathered += [partner] + [tp_move(partner, 4 - r) for r in (1, 2, 3)]
    w, masked = load_weights(mask_row, wq, wk, wv)
    kv, kvn, all_rows = project_keys(gathered, w, masked, cosine, sine)

    def along(step):
        return lambda y, z, c: (y, (z + (NZ - step if c else step)) % NZ, c)

    pair = jnp.stack([kv, swap(kv)])
    two = ctx_move(pair, along(2))
    one = ctx_move(pair, along(1))
    three = ctx_move(two, along(1))
    half = ctx_move(two[0], along(2))
    q = project_queries(all_rows, w, masked, cosine, sine)
    far = ctx_move(q, lambda y, z, c: (0, z, c) if y == 1 else None)
    queries = (q, swap(q), far, swap(far))

    up_mine, up_other, low_mine, low_other = early(table, *queries, pair, two, one, kvn)
    mine, other = late(1, table, *queries, three, half, up_mine, up_other, kvn)
    upper = merge_cores(mine, swap(other))
    returned = ctx_move(upper, lambda y, z, c: (1, z, c) if y == 0 else None)
    mine, other = late(0, table, *queries, three, half, low_mine, low_other, upper)
    lower = merge_cores(mine, swap(other))
    terms = list(output(upper, lower, returned, w_out))
    if TERMS_PP:
        for r in range(1, NT):
            terms[r] = tp_move(terms[r], r)
    else:
        terms = [lax.all_to_all(terms[0], "tp", 0, 0)]
    return sum_terms(terms)


def solution(mesh):
    return jax.shard_map(
        layer,
        mesh=mesh,
        in_specs=(
            P(("ctx", "tp"), None),
            P(("ctx", "tp")),
            P(),
            P(),
            P(None, "tp"),
            P(None, "tp"),
            P(None, "tp"),
            P("tp", None),
            P(),
        ),
        out_specs=(P(("ctx", "tp"), None), P(("ctx", "tp"), None)),
        check_vma=False,
    )
```

```python
import jax
import jax.numpy as jnp
from jax import lax
from jax.experimental import pallas as pl
from jax.experimental.pallas import tpu as pltpu
from jax.sharding import PartitionSpec as P


HEAD_DIM = 128
BLOCK = 32
ROPE_BASE = 500000.0
EPSILON = 1e-05
TOK = 128
D = 4096
NZ = 8
NT = 8
LOG2E = 1.4426950408889634
SCALE2 = HEAD_DIM ** (-0.5) * LOG2E
HIDDEN = -1e30
FLOOR = -1e29
TERMS_PP = True


VMEM = pl.BlockSpec(memory_space=pltpu.VMEM)
ANY = pl.BlockSpec(memory_space=pl.ANY)
HBM = pl.BlockSpec(memory_space=pltpu.HBM)
SMEM = pl.BlockSpec(memory_space=pltpu.SMEM)


def params(mib=16):
    return pltpu.CompilerParams(vmem_limit_bytes=mib << 20)


def cost(mib, flops=1 << 20):
    return pl.CostEstimate(flops=flops, bytes_accessed=mib << 20, transcendentals=0)


def struct(*shape, dtype=jnp.bfloat16):
    return jax.ShapeDtypeStruct(shape, dtype)


def head(h):
    return slice(h * HEAD_DIM, (h + 1) * HEAD_DIM)


def relative(me, r):
    return ((me // 4) ^ (r // 4)) * 4 + (me + r) % 4


def norm_kernel(tok_hbm, flag_hbm, mask_hbm, gain_hbm, out_ref, mask_out_ref, tok, flag, mask, gain, sems):
    copies = [
        pltpu.make_async_copy(src, dst, sems.at[i])
        for i, (src, dst) in enumerate(
            ((tok_hbm, tok), (flag_hbm, flag), (mask_hbm, mask), (gain_hbm, gain))
        )
    ]
    for copy in copies:
        copy.start()
    for copy in copies:
        copy.wait()
    wide_gain = gain[...].astype(jnp.float32)
    row = lax.broadcasted_iota(jnp.int32, (16, 128), 0)
    flags = jnp.zeros((16, 128), jnp.float32)
    for i in range(16):
        flags = jnp.where(row == i, flag[i].astype(jnp.float32), flags)
    out_ref[:, D:] = flags.astype(jnp.bfloat16)
    wide = tok[...].astype(jnp.float32)
    factor = lax.rsqrt(jnp.mean(wide * wide, axis=-1, keepdims=True) + EPSILON)
    wide_mask = mask[...].astype(jnp.float32)
    square = jnp.sum(wide_mask * wide_mask, axis=0, keepdims=True)
    factor_mask = lax.rsqrt(jnp.sum(square, axis=1, keepdims=True) / D + EPSILON)
    mask_row = wide_mask * factor_mask * wide_gain
    for j in range(D // 128):
        lanes = slice(j * 128, (j + 1) * 128)
        out_ref[:, lanes] = (wide[:, lanes] * factor * wide_gain[j : j + 1]).astype(jnp.bfloat16)
        mask_out_ref[:, lanes] = jnp.broadcast_to(mask_row[j : j + 1], (16, 128)).astype(jnp.bfloat16)


def norm(tokens, flags, mask_embed, gain):
    return pl.pallas_call(
        norm_kernel,
        out_shape=(struct(16, D + 128), struct(16, D)),
        in_specs=[HBM] * 4,
        out_specs=(VMEM, VMEM),
        scratch_shapes=[
            pltpu.VMEM((16, D), jnp.bfloat16),
            pltpu.SMEM((16,), jnp.int32),
            pltpu.VMEM((D // 128, 128), jnp.bfloat16),
            pltpu.VMEM((D // 128, 128), jnp.bfloat16),
            pltpu.SemaphoreType.DMA((4,)),
        ],
        compiler_params=pltpu.CompilerParams(vmem_limit_bytes=16 << 20),
        cost_estimate=cost(1),
        name="norm",
    )(*(pltpu.with_memory_space_constraint(v, pltpu.HBM) for v in (tokens, flags, mask_embed.reshape(D // 128, 128), gain.reshape(D // 128, 128))))


def weights_kernel(mask_ref, wq_hbm, wk_hbm, wv_hbm, w_ref, masked_ref, sems):
    parts = 4
    depth = D // parts
    copies = []
    for i, src in enumerate((wk_hbm, wv_hbm, wq_hbm)):
        for p in range(parts):
            rows = pl.ds(p * depth, depth)
            copies.append(
                pltpu.make_async_copy(src.at[rows, :], w_ref.at[rows, pl.ds(i * 256, 256)], sems.at[i, p])
            )
    for copy in copies:
        copy.start()
    for copy in copies:
        copy.wait()
    for i in range(3):
        masked_ref[:, i * 256 : (i + 1) * 256] = jnp.dot(
            mask_ref[...], w_ref[:, i * 256 : (i + 1) * 256], preferred_element_type=jnp.float32
        )[:8]


def load_weights(mask_row, wq, wk, wv):
    return pl.pallas_call(
        weights_kernel,
        out_shape=(struct(D, 768), struct(8, 768, dtype=jnp.float32)),
        in_specs=[VMEM, HBM, HBM, HBM],
        out_specs=(VMEM, VMEM),
        scratch_shapes=[pltpu.SemaphoreType.DMA((3, 4))],
        compiler_params=pltpu.CompilerParams(vmem_limit_bytes=16 << 20),
        cost_estimate=cost(12),
        name="weights",
    )(mask_row, *(pltpu.with_memory_space_constraint(w, pltpu.HBM) for w in (wq, wk, wv)))


def place():
    ctx = lax.axis_index("ctx")
    return ctx // 16, (ctx // 2) % NZ, ctx % 2


def rotary(v, cosine, sine):
    return v * cosine + pltpu.roll(v, HEAD_DIM // 2, 1) * sine


def both(rows_ref, w_ref, masked_ref, i):
    cols = slice(i * 256, (i + 1) * 256)
    noisy = rows_ref[:, D : D + 1].astype(jnp.float32) > 0.5
    clean = jnp.dot(rows_ref[:, :D], w_ref[:, cols], preferred_element_type=jnp.float32)
    return clean, jnp.where(noisy, masked_ref[0:1, cols], clean)


def key_kernel(*refs):
    g_refs = refs[:NT]
    w_ref, masked_ref, cos_ref, sin_ref, kv_ref, kvn_ref, rows_ref = refs[NT:]
    me = lax.axis_index("tp")
    for r in range(NT):
        rows_ref[pl.ds(pl.multiple_of(relative(me, r) * 16, 16), 16), :] = g_refs[r][...]
    cosine, sine = cos_ref[...], sin_ref[...]
    keys = both(rows_ref, w_ref, masked_ref, 0)
    values = both(rows_ref, w_ref, masked_ref, 1)
    for h in range(2):
        for k, v, ref in zip(keys, values, (kv_ref, kvn_ref)):
            ref[head(h), :] = rotary(k[:, head(h)], cosine, sine).T.astype(jnp.bfloat16)
            ref[head(2 + h), :] = v[:, head(h)].astype(jnp.bfloat16)


def project_keys(gathered, w, masked, cosine, sine):
    return pl.pallas_call(
        key_kernel,
        out_shape=(struct(512, TOK), struct(512, TOK), struct(TOK, D + 128)),
        in_specs=[VMEM] * (NT + 4),
        out_specs=(VMEM,) * 3,
        compiler_params=params(),
        cost_estimate=cost(6, 1 << 30),
        name="keys",
    )(*gathered, w, masked, cosine, sine)


def query_kernel(rows_ref, w_ref, masked_ref, cos_ref, sin_ref, q_ref):
    cosine, sine = cos_ref[...], sin_ref[...]
    for i, q in enumerate(both(rows_ref, w_ref, masked_ref, 2)):
        for h in range(2):
            q_ref[i * TOK : (i + 1) * TOK, head(h)] = rotary(q[:, head(h)], cosine, sine).astype(jnp.bfloat16)


def project_queries(rows, w, masked, cosine, sine):
    return pl.pallas_call(
        query_kernel,
        out_shape=struct(2 * TOK, 256),
        in_specs=[VMEM] * 5,
        out_specs=VMEM,
        compiler_params=params(),
        cost_estimate=cost(3, 1 << 29),
        name="queries",
    )(rows, w, masked, cosine, sine)


def pack_stats(lses):
    rows = lses[0].shape[0]
    lane = lax.broadcasted_iota(jnp.int32, (rows, 128), 1)
    total = jnp.zeros((rows, 128), jnp.float32)
    for h, lse in enumerate(lses):
        rest = lse
        for part in range(3):
            piece = rest.astype(jnp.bfloat16).astype(jnp.float32)
            total = jnp.where(lane == h * 4 + part, piece, total)
            rest = rest - piece
    return total.astype(jnp.bfloat16)


def unpack_stats(block):
    wide = block.astype(jnp.float32)
    return [
        wide[:, h * 4 : h * 4 + 1] + wide[:, h * 4 + 1 : h * 4 + 2] + wide[:, h * 4 + 2 : h * 4 + 3]
        for h in range(2)
    ]


def unpack(ref):
    block = ref[...]
    return [block[:, head(h)].astype(jnp.float32) for h in range(2)], unpack_stats(block[:, 256:])


def pack(part, ref):
    outs, lses = part
    for h in range(2):
        ref[:, head(h)] = outs[h].astype(jnp.bfloat16)
    ref[:, 256:] = pack_stats(lses)


def merge(a, b):
    outs, lses = [], []
    for h in range(2):
        peak = jnp.maximum(a[1][h], b[1][h])
        wa, wb = jnp.exp2(a[1][h] - peak), jnp.exp2(b[1][h] - peak)
        total = wa + wb
        outs.append((a[0][h] * wa + b[0][h] * wb) / total)
        lses.append(peak + jnp.log2(total))
    return outs, lses


TILES = ((0, 0), (2, 0), (2, 1), (1, 0), (1, 1), (3, 0), (3, 1), (4, 0))
EARLY = TILES[:5]
LATE = TILES[5:]


def tile_block(tile, y, z, c):
    step, flip = tile
    source = (z + jnp.where(c == 0, NZ - step, step)) % NZ
    core = 1 - c if flip else c
    return (y * 16 + source * 2 + core) * 4


def held_shapes(tiles):
    length = len(tiles) * TOK
    return [pltpu.VMEM((256, length), jnp.bfloat16), pltpu.VMEM((2, length, HEAD_DIM), jnp.bfloat16)]


def gather_keys(blocks, keys, values):
    for i, block in enumerate(blocks):
        cols = slice(i * TOK, (i + 1) * TOK)
        keys[:, cols] = block[:256]
        for h in range(2):
            values[h, cols, :] = block[256 + h * HEAD_DIM : 256 + (h + 1) * HEAD_DIM]


def partial(q, held, tiles, table_ref, yq, cq, near=None):
    y, z, c = place()
    keys, values = held
    col = lax.broadcasted_iota(jnp.int32, (1, len(tiles) * TOK), 1)
    key_block = (col % TOK) // BLOCK
    for i, tile in enumerate(tiles):
        key_block = jnp.where(col // TOK == i, key_block + tile_block(tile, y, z, c), key_block)
    part = lax.broadcasted_iota(jnp.int32, (8, 1), 0)
    first = (yq * 16 + z * 2 + cq) * 4
    low = jnp.zeros((8, 1), jnp.int32)
    high = jnp.zeros((8, 1), jnp.int32)
    for p in range(8):
        copy, block = p // 4, first + p % 4
        low = jnp.where(part == p, table_ref[copy, block], low)
        high = jnp.where(part == p, block - copy, high)
    hide = jnp.where((key_block >= low) & (key_block <= high), 0.0, HIDDEN)
    hide = jnp.broadcast_to(hide[:, None, :], (8, BLOCK, len(tiles) * TOK)).reshape(2 * TOK, len(tiles) * TOK)
    outs, lses = [], []
    for h in range(2):
        qh = q[:, head(h)]
        scores = jnp.dot(qh, keys[head(h), :], preferred_element_type=jnp.float32) * SCALE2 + hide
        peak = jnp.maximum(jnp.max(scores, axis=-1, keepdims=True), FLOOR)
        if near is not None:
            kvn_ref, wanted = near
            own = jnp.dot(qh[TOK:], kvn_ref[head(h), :], preferred_element_type=jnp.float32) * SCALE2
            same = (
                lax.broadcasted_iota(jnp.int32, (TOK, TOK), 0) // BLOCK
                == lax.broadcasted_iota(jnp.int32, (TOK, TOK), 1) // BLOCK
            ) & wanted
            own = jnp.where(same, own, HIDDEN)
            peak_own = jnp.maximum(peak[TOK:], jnp.max(own, axis=-1, keepdims=True))
            peak = jnp.concatenate([peak[:TOK], peak_own], axis=0)
        weights = jnp.exp2(scores - peak)
        total = jnp.sum(weights, axis=-1, keepdims=True)
        weighted = jnp.dot(
            weights.astype(jnp.bfloat16), values[h], preferred_element_type=jnp.float32
        )
        if near is not None:
            wown = jnp.exp2(own - peak_own)
            total = total + jnp.concatenate(
                [jnp.zeros((TOK, 1), jnp.float32), jnp.sum(wown, axis=-1, keepdims=True)], axis=0
            )
            extra = jnp.dot(
                wown.astype(jnp.bfloat16), kvn_ref[head(2 + h), :], preferred_element_type=jnp.float32
            )
            weighted = weighted + jnp.concatenate(
                [jnp.zeros((TOK, HEAD_DIM), jnp.float32), extra], axis=0
            )
        some = total > 0.0
        safe = jnp.where(some, total, 1.0)
        outs.append(weighted / safe)
        lses.append(jnp.where(some, peak + jnp.log2(safe), FLOOR))
    return outs, lses


def save(part, ref):
    outs, lses = part
    for h in range(2):
        ref[:, head(h)] = outs[h]
        ref[:, head(2 + h)] = jnp.broadcast_to(lses[h], (2 * TOK, HEAD_DIM))


def saved(ref):
    return [ref[:, head(h)] for h in range(2)], [ref[:, (2 + h) * 128 : (2 + h) * 128 + 1] for h in range(2)]


def early_kernel(table_ref, q_ref, other_ref, far_ref, far_other_ref, own_ref, two_ref, one_ref, kvn_ref,
                 up_mine, up_other, low_mine, low_other, keys, values):
    y, _, c = place()
    gather_keys((own_ref[0], two_ref[0], two_ref[1], one_ref[0], one_ref[1]), keys, values)
    keys = (keys, values)
    tiles = EARLY
    mine = jnp.where(y == 1, q_ref[...], far_ref[...])
    other = jnp.where(y == 1, other_ref[...], far_other_ref[...])
    save(partial(mine, keys, tiles, table_ref, 1, c, (kvn_ref, y == 1)), up_mine)
    save(partial(other, keys, tiles, table_ref, 1, 1 - c), up_other)

    @pl.when(y == 0)
    def _():
        save(partial(q_ref[...], keys, tiles, table_ref, 0, c, (kvn_ref, y == 0)), low_mine)
        save(partial(other_ref[...], keys, tiles, table_ref, 0, 1 - c), low_other)

    @pl.when(y == 1)
    def _():
        low_mine[...] = jnp.zeros_like(low_mine)
        low_other[...] = jnp.zeros_like(low_other)


def early(table, q, other, far, far_other, own, two, one, kvn):
    return pl.pallas_call(
        early_kernel,
        out_shape=(struct(2 * TOK, 512, dtype=jnp.float32),) * 4,
        in_specs=[SMEM] + [VMEM] * 8,
        out_specs=(VMEM,) * 4,
        scratch_shapes=held_shapes(EARLY),
        compiler_params=params(),
        cost_estimate=cost(4, 1 << 29),
        name="early",
    )(table, q, other, far, far_other, own, two, one, kvn)


def late_kernel(line, flip, table_ref, q_ref, far_ref, three_ref, half_ref, early_ref, _, out_ref, keys, values):
    y, _, c = place()

    def work():
        gather_keys((three_ref[0], three_ref[1], half_ref[...]), keys, values)
        q = jnp.where(y == 1, q_ref[...], far_ref[...]) if line == 1 else q_ref[...]
        core = 1 - c if flip else c
        pack(merge(saved(early_ref), partial(q, (keys, values), LATE, table_ref, line, core)), out_ref)

    if line == 1:
        work()
    else:
        pl.when(y == 0)(work)

        @pl.when(y == 1)
        def _():
            out_ref[...] = jnp.zeros_like(out_ref)


def late(line, flip, table, q, far, three, half, before, after):
    def kernel(*refs):
        late_kernel(line, flip, *refs)

    return pl.pallas_call(
        kernel,
        out_shape=struct(2 * TOK, 384),
        in_specs=[SMEM] + [VMEM] * 5 + [ANY],
        out_specs=VMEM,
        scratch_shapes=held_shapes(LATE),
        compiler_params=params(),
        cost_estimate=cost(2, 1 << 28),
    )(table, q, far, three, half, before, after)


def merge_kernel(mine_ref, swap_ref, out_ref):
    pack(merge(unpack(mine_ref), unpack(swap_ref)), out_ref)


def merge_cores(mine, swapped):
    return pl.pallas_call(
        merge_kernel,
        out_shape=struct(2 * TOK, 384),
        in_specs=[VMEM, VMEM],
        out_specs=VMEM,
        compiler_params=params(),
        cost_estimate=cost(1),
        name="merge",
    )(mine, swapped)


def output_kernel(upper_ref, lower_ref, far_ref, w_ref, *refs):
    att = refs[-1]
    outs, _ = merge(unpack(upper_ref), unpack(far_ref))
    upper_line = place()[0] == 1
    lower, _ = unpack(lower_ref)
    for h in range(2):
        value = jnp.where(upper_line, outs[h], lower[h]).astype(jnp.bfloat16)
        for t in range(NT):
            for s in range(2):
                att[t, s * 16 : (s + 1) * 16, head(h)] = value[s * TOK + t * 16 : s * TOK + (t + 1) * 16]
    me = lax.axis_index("tp")
    if TERMS_PP:
        rows = jnp.concatenate([att[relative(me, r)] for r in range(NT)], axis=0)
    else:
        rows = att[...].reshape(2 * TOK, 256)
    for i in range(8):
        cols = slice(i * 512, (i + 1) * 512)
        terms = jnp.dot(rows, w_ref[:, cols], preferred_element_type=jnp.float32).astype(jnp.bfloat16)
        if TERMS_PP:
            for r in range(NT):
                refs[r][:, cols] = terms[r * 32 : (r + 1) * 32]
        else:
            refs[0][:, :, cols] = terms.reshape(NT, 32, 512)


def output(upper, lower, far, w_out):
    shapes = (struct(32, D),) * NT if TERMS_PP else (struct(NT, 32, D),)
    return pl.pallas_call(
        output_kernel,
        out_shape=shapes,
        in_specs=[VMEM] * 4,
        out_specs=(VMEM,) * len(shapes),
        scratch_shapes=[pltpu.VMEM((NT, 32, 256), jnp.bfloat16)],
        compiler_params=params(),
        cost_estimate=cost(4, 1 << 29),
        name="terms",
    )(upper, lower, far, w_out)


def sum_kernel(*refs):
    clean_ref, noisy_ref = refs[-2:]
    blocks = refs[:-2]
    total = 0.0
    for t in range(NT):
        block = blocks[t][...] if TERMS_PP else blocks[0][t]
        total = total + block.astype(jnp.float32)
    clean_ref[...] = total[:16].astype(jnp.bfloat16)
    noisy_ref[...] = total[16:].astype(jnp.bfloat16)


def sum_terms(blocks):
    return pl.pallas_call(
        sum_kernel,
        out_shape=(struct(16, D), struct(16, D)),
        in_specs=[VMEM] * len(blocks),
        out_specs=(VMEM, VMEM),
        compiler_params=params(),
        cost_estimate=cost(2),
        name="sum_terms",
    )(*blocks)


def ctx_perm(move):
    pairs = []
    for y in range(2):
        for z in range(NZ):
            for c in range(2):
                target = move(y, z, c)
                if target is not None:
                    ty, tz, tc = target
                    pairs.append((y * 16 + z * 2 + c, ty * 16 + tz * 2 + tc))
    return pairs


def ctx_move(x, move):
    return lax.ppermute(x, "ctx", ctx_perm(move))


def swap(x):
    return ctx_move(x, lambda y, z, c: (y, z, 1 - c))


def tp_move(x, r):
    return lax.ppermute(x, "tp", [(i, relative(i, r)) for i in range(NT)])


def tables(positions):
    half = HEAD_DIM // 2
    freqs = ROPE_BASE ** (-2.0 * jnp.arange(half).astype(jnp.float32) / HEAD_DIM)
    angles = positions.astype(jnp.float32)[:, None] * freqs[None, :]
    cosine, sine = jnp.cos(angles), jnp.sin(angles)
    return jnp.concatenate([cosine, cosine], 1), jnp.concatenate([-sine, sine], 1)


def layer(tokens, flags, mask_embed, gain, wq, wk, wv, w_out, block_mask):
    ctx = lax.axis_index("ctx")
    cosine, sine = tables(ctx * TOK + jnp.arange(TOK, dtype=jnp.int32))
    blocks = jnp.arange(block_mask.shape[0], dtype=jnp.int32)
    table = jnp.stack(
        [
            blocks + 1 - jnp.sum(block_mask % 2, axis=1),
            blocks - jnp.sum(block_mask // 2, axis=1),
        ]
    ).astype(jnp.int32)

    rows, mask_row = norm(tokens, flags, mask_embed, gain)
    partner = tp_move(rows, 4)
    gathered = [rows] + [tp_move(rows, 4 - r) for r in (1, 2, 3)]
    gathered += [partner] + [tp_move(partner, 4 - r) for r in (1, 2, 3)]
    w, masked = load_weights(mask_row, wq, wk, wv)
    kv, kvn, all_rows = project_keys(gathered, w, masked, cosine, sine)

    def along(step):
        return lambda y, z, c: (y, (z + (NZ - step if c else step)) % NZ, c)

    pair = jnp.stack([kv, swap(kv)])
    two = ctx_move(pair, along(2))
    one = ctx_move(pair, along(1))
    three = ctx_move(two, along(1))
    half = ctx_move(two[0], along(2))
    q = project_queries(all_rows, w, masked, cosine, sine)
    far = ctx_move(q, lambda y, z, c: (0, z, c) if y == 1 else None)
    queries = (q, swap(q), far, swap(far))

    up_mine, up_other, low_mine, low_other = early(table, *queries, pair, two, one, kvn)
    q, q_other, q_far, q_far_other = queries
    other = late(1, True, table, q_other, q_far_other, three, half, up_other, kvn)
    other_back = swap(other)
    upper = merge_cores(late(1, False, table, q, q_far, three, half, up_mine, other), other_back)
    returned = ctx_move(upper, lambda y, z, c: (1, z, c) if y == 0 else None)
    other = late(0, True, table, q_other, q_far_other, three, half, low_other, upper)
    other_back = swap(other)
    lower = merge_cores(late(0, False, table, q, q_far, three, half, low_mine, other), other_back)
    terms = list(output(upper, lower, returned, w_out))
    if TERMS_PP:
        for r in range(1, NT):
            terms[r] = tp_move(terms[r], r)
    else:
        terms = [lax.all_to_all(terms[0], "tp", 0, 0)]
    return sum_terms(terms)


def solution(mesh):
    return jax.shard_map(
        layer,
        mesh=mesh,
        in_specs=(
            P(("ctx", "tp"), None),
            P(("ctx", "tp")),
            P(),
            P(),
            P(None, "tp"),
            P(None, "tp"),
            P(None, "tp"),
            P("tp", None),
            P(),
        ),
        out_specs=(P(("ctx", "tp"), None), P(("ctx", "tp"), None)),
        check_vma=False,
    )
```
